1024 devices in a mesh: ctx: 128 (over y, z), head: 8 (over x, core).
Axes of the slice: x: 4, y: 8, z: 16, core: 2. Of those that a mesh axis runs over, the one named last changes fastest.
Arguments:
- seq_inputs: bfloat16 [32768, 5120], P('ctx', 'head'), may hold values from -0.4375 to 0.4375
- state_write: bfloat16 [32768, 128], P('ctx'), may hold values from -2 to 2
- state_read: bfloat16 [32768, 128], P('ctx'), may hold values from -2 to 2
- log_decay: float32 [80, 32768], P('head', 'ctx'), may hold values from -1 to 0
- level_weight: int32 [8, 80, 32768], P(None, 'head', 'ctx'), may hold values from 1 to 16
- grad_out: bfloat16 [32768, 5120], P('ctx', 'head'), may hold values from -0.4375 to 0.4375
Outputs:
- mixer_out: bfloat16 [32768, 5120], P('ctx', 'head')
- grad_inputs: bfloat16 [32768, 5120], P('ctx', 'head')
- grad_write: float32 [32768, 128], P(('ctx', 'head'))
- grad_read: float32 [32768, 128], P(('ctx', 'head'))
The draws below stay inside these ranges and needn't reach their ends.
All inputs are finite; a program needn't handle non-finite values.
Results may differ from the reference program's by a relative error of at most 0.0064.
Values sent between devices are 32-bit elements; how exact they have to be, the bound alone decides.
No kernel may reach another device: no remote copies, remote signals or barrier semaphores. Data moves between devices by JAX's collectives and lax.ppermute only.
A program may use at most 32 MiB of HBM per device.

```python
import math
import jax
import jax.numpy as jnp
from jax import lax

HEAD_TOTAL = 80
P_SIZE = 64
N = 128
TOK_DEV = 256
LEVELS = 8
TOKEN_TOTAL = 32768
N_CTX = 128


def draw_log_decay(key, part):
    key_rows = jax.random.split(key, 7)
    fast_share = 0.5
    stretch_count = TOKEN_TOTAL // TOK_DEV
    fast_heads = jax.random.uniform(key_rows[0], (HEAD_TOTAL, 1)) < fast_share
    fast_rate = 1.0 / jax.random.uniform(key_rows[1], (HEAD_TOTAL, 1), minval=30.0, maxval=50.0)
    slow_rate = 1.15 / TOKEN_TOTAL * jax.random.uniform(key_rows[2], (HEAD_TOTAL, 1), minval=0.5, maxval=1.0)
    baseline_decay_rate = jnp.where(fast_heads, fast_rate, slow_rate)
    segment_multiplier = jnp.exp(jax.random.uniform(key_rows[3], (HEAD_TOTAL, stretch_count, 1), minval=math.log(0.5), maxval=0.0))
    segment_multiplier = jnp.broadcast_to(segment_multiplier, (HEAD_TOTAL, stretch_count, TOK_DEV)).reshape(HEAD_TOTAL, TOKEN_TOTAL)
    token_multiplier = jnp.exp(jax.random.uniform(key_rows[4], (HEAD_TOTAL, TOKEN_TOTAL), minval=math.log(0.5), maxval=0.0))
    spike_locations = jax.random.randint(key_rows[5], (HEAD_TOTAL, 2), 0, TOKEN_TOTAL)
    spike_level_depth = jax.random.uniform(key_rows[6], (HEAD_TOTAL, 2), minval=0.22, maxval=0.45)
    token_positions = jnp.arange(TOKEN_TOTAL)
    spike_mask = (token_positions[None, None, :] == spike_locations[:, :, None]).astype(jnp.float32)
    spike_events = jnp.sum(spike_mask * spike_level_depth[:, :, None], axis=1)
    return -(baseline_decay_rate * segment_multiplier * token_multiplier + spike_events)


def place_ends(values, stream_key, low, top_value):
    extent = values.shape
    place = [jax.random.randint(jax.random.fold_in(stream_key, axis), (), 0, extent[axis]) for axis in range(len(extent))]
    values = values.at[tuple(place)].set(low)
    longest = extent.index(max(extent))
    place[longest] = (place[longest] + 1) % extent[longest]
    return values.at[tuple(place)].set(top_value)


def steps_of(rng, shape, shards, least, top_value):
    factor_of, own = 1.0, jax.random.fold_in(rng, 6)
    for position, shards_of in shards:
        steps = jnp.exp(jax.random.uniform(jax.random.fold_in(own, position), (shards_of,), jnp.float32, least / len(shards), top_value / len(shards)))
        factor_of = factor_of * jnp.repeat(steps, shape[position] // shards_of).reshape([-1 if axis == position else 1 for axis in range(len(shape))])
    return factor_of


def bell_draw(own_key, dims, deviation, limit, cuts=(), kind=jnp.bfloat16):
    array = jax.random.normal(own_key, dims, jnp.float32) * deviation
    if len(cuts) > 0:
        array = steps_of(own_key, dims, cuts, -0.22, 0.18) * array
    return jnp.clip(array, min=-limit, max=limit).astype(kind)


def setup_inputs(seed: int = 0) -> dict:
    keys = jax.random.split(jax.random.key(seed), 7)
    return {
        "seq_inputs": bell_draw(keys[0], (TOKEN_TOTAL, HEAD_TOTAL * P_SIZE), 0.03, 0.4375, ((0, 128), (1, 8))),
        "state_write": bell_draw(keys[1], (TOKEN_TOTAL, N), 0.15, 2.0, ((0, 128),)),
        "state_read": bell_draw(keys[2], (TOKEN_TOTAL, N), 0.15, 2.0, ((0, 128),)),
        "log_decay": draw_log_decay(jax.random.fold_in(keys[6], 71), 0),
        "level_weight": place_ends(jax.random.randint(keys[4], (LEVELS, HEAD_TOTAL, TOKEN_TOTAL), 1, 17), jax.random.fold_in(keys[4], 1), 1, 16).astype(jnp.int32),
        "grad_out": bell_draw(keys[5], (TOKEN_TOTAL, HEAD_TOTAL * P_SIZE), 0.03, 0.4375, ((0, 128), (1, 8))),
    }


def stretch_local(packed):
    inputs, writes, reads, decays, weights, cotangent = packed
    running = jnp.cumsum(decays, axis=1)
    ending = running[:, -1]
    scores = jnp.dot(reads, writes.T, preferred_element_type=jnp.float32)
    token_positions = jnp.arange(TOK_DEV)
    causal = (token_positions[:, None] >= token_positions[None, :])[None]
    gaps = running[:, :, None] - running[:, None, :]
    local_weight = jnp.where(causal, jnp.exp(jnp.where(causal, gaps, 0.0)), 0.0) * weights[:, :, None]
    mixing = (local_weight * scores[None]).astype(jnp.bfloat16)
    inputs_wide = inputs.astype(jnp.float32)
    cot_wide = cotangent.astype(jnp.float32)
    mixing_wide = mixing.astype(jnp.float32)
    y_local = jnp.einsum('htu,uhp->thp', mixing_wide, inputs_wide)
    d_mixing = jnp.einsum('thp,uhp->htu', cot_wide, inputs_wide)
    d_scores = (d_mixing * local_weight).astype(jnp.bfloat16).astype(jnp.float32)
    dread_local = jnp.einsum('htu,un->tn', d_scores, writes.astype(jnp.float32))
    dwrite_local = jnp.einsum('htu,tn->un', d_scores, reads.astype(jnp.float32))
    dinput_local = jnp.einsum('htu,thp->uhp', mixing_wide, cot_wide)
    to_end = jnp.exp(ending[:, None] - running)
    written = (to_end[:, :, None] * writes.astype(jnp.float32)[None]).astype(jnp.bfloat16)
    state = jnp.einsum('uhp,hun->hpn', inputs_wide, written.astype(jnp.float32))
    return y_local, dinput_local, dread_local, dwrite_local, state, running


def far_level(packed):
    reads, cotangent, coeff, bucket = packed
    bucket_wide = bucket.astype(jnp.float32)
    coeff_rows = coeff.T[:, :, None]
    raw = jnp.einsum('tn,hpn->thp', reads.astype(jnp.float32), bucket_wide, precision=lax.Precision.HIGHEST)
    y_part = raw * coeff_rows
    weighted = (coeff_rows * cotangent.astype(jnp.float32)).astype(jnp.bfloat16).astype(jnp.float32)
    dread_part = jnp.einsum('thp,hpn->tn', weighted, bucket_wide, precision=lax.Precision.HIGHEST)
    dbucket = jnp.einsum('thp,tn->hpn', weighted, reads.astype(jnp.float32))
    return y_part, dread_part, dbucket


def state_grads(packed):
    inputs, writes, running, dstate_low = packed
    to_end = jnp.exp(running[:, -1:] - running)
    written = (to_end[:, :, None] * writes.astype(jnp.float32)[None]).astype(jnp.bfloat16)
    dstate_wide = dstate_low.astype(jnp.float32)
    dinput_far = jnp.einsum('hpn,hun->uhp', dstate_wide, written.astype(jnp.float32))
    per_head = jnp.einsum('hpn,uhp->uhn', dstate_wide, inputs.astype(jnp.float32))
    dwrite_far = jnp.sum(to_end.T[:, :, None] * per_head, axis=1)
    return dinput_far, dwrite_far


def reference(seq_inputs, state_write, state_read, log_decay, level_weight, grad_out):
    stretch_count = N_CTX
    depth = stretch_count.bit_length() - 1
    inputs = seq_inputs.reshape(stretch_count, TOK_DEV, HEAD_TOTAL, P_SIZE)
    cotangent = grad_out.reshape(stretch_count, TOK_DEV, HEAD_TOTAL, P_SIZE)
    writes = state_write.reshape(stretch_count, TOK_DEV, N)
    reads = state_read.reshape(stretch_count, TOK_DEV, N)
    decays = log_decay.reshape(HEAD_TOTAL, stretch_count, TOK_DEV).transpose(1, 0, 2)
    scaled = level_weight.astype(jnp.float32) * 0.125
    scaled = scaled.reshape(LEVELS, HEAD_TOTAL, stretch_count, TOK_DEV).transpose(2, 0, 1, 3)
    y_local, dinput_local, dread_local, dwrite_local, states, running = lax.map(
        stretch_local, (inputs, writes, reads, decays, scaled[:, 0], cotangent))
    spans = [running[:, :, -1]]
    blocks = [states]
    for level_bit in range(depth):
        prior_block = blocks[-1]
        prior_span = spans[-1]
        blocks.append(jnp.exp(prior_span[1::2])[:, :, None, None] * prior_block[0::2] + prior_block[1::2])
        spans.append(prior_span[0::2] + prior_span[1::2])
    stretch_ids = jnp.arange(stretch_count)
    offset = jnp.zeros((stretch_count, HEAD_TOTAL), running.dtype)
    y_far = jnp.zeros_like(y_local)
    dread_far = jnp.zeros_like(dread_local)
    sibling_sums = []
    for level_bit in range(depth):
        bit_set = (stretch_ids // (2 ** level_bit)) % 2
        partner = stretch_ids // (2 ** level_bit) + 1 - 2 * bit_set
        bucket = blocks[level_bit][partner]
        is_set = (bit_set == 1)
        coeff = jnp.where(is_set[:, None, None], scaled[:, level_bit + 1] * jnp.exp(running + offset[:, :, None]), 0.0)
        y_part, dread_part, dbucket = lax.map(far_level, (reads, cotangent, coeff, bucket))
        y_far = y_far + y_part
        dread_far = dread_far + dread_part
        grouped = dbucket.reshape(stretch_count // (2 ** level_bit), 2 ** level_bit, HEAD_TOTAL, P_SIZE, N).sum(axis=1)
        sibling_sums.append(grouped[1::2])
        offset = offset + jnp.where(is_set[:, None], spans[level_bit][partner], 0.0)
    carried = jnp.zeros((1, HEAD_TOTAL, P_SIZE, N), running.dtype)
    for level_bit in reversed(range(depth)):
        left_part = jnp.exp(spans[level_bit][1::2])[:, :, None, None] * carried + sibling_sums[level_bit]
        carried = jnp.stack([left_part, carried], axis=1).reshape(-1, HEAD_TOTAL, P_SIZE, N)
    dstate_low = carried.astype(jnp.bfloat16)
    dinput_far, dwrite_far = lax.map(state_grads, (inputs, writes, running, dstate_low))
    mixer_out = (y_local + y_far).astype(jnp.bfloat16).reshape(TOKEN_TOTAL, HEAD_TOTAL * P_SIZE)
    grad_inputs = (dinput_local + dinput_far).astype(jnp.bfloat16).reshape(TOKEN_TOTAL, HEAD_TOTAL * P_SIZE)
    grad_write = (dwrite_local + dwrite_far).reshape(TOKEN_TOTAL, N)
    grad_read = (dread_local + dread_far).reshape(TOKEN_TOTAL, N)
    return mixer_out, grad_inputs, grad_write, grad_read
```

```python
import jax
import jax.numpy as jnp
from jax import lax
from jax.sharding import PartitionSpec as P


def exchange(value, bit):
    pairs = [(source, source ^ 2**bit) for source in range(lax.axis_size("ctx"))]
    return lax.ppermute(value, "ctx", pairs)


def to_left(value):
    pairs = [(source, source - 1) for source in range(1, lax.axis_size("ctx"), 2)]
    return lax.ppermute(value, "ctx", pairs)


def sum_at_owner(value, axis):
    pieces = value.reshape(lax.axis_size(axis), -1, value.shape[1])
    return lax.all_to_all(pieces, axis, split_axis=0, concat_axis=0, tiled=True).sum(axis=0)


def block_spans(total, shard_index, level_count):
    size = 2**level_count
    mine = jnp.broadcast_to(total[None, None, :], (size, 1, total.shape[0]))
    spans = lax.all_to_all(mine, "ctx", split_axis=0, concat_axis=0, tiled=True)
    spans = spans[:, 0]
    stretch = jnp.arange(size)[:, None]
    own_spans, peer_spans, offsets = ([], [], [])
    offset = jnp.zeros_like(total)
    for bit in range(level_count):
        block = shard_index // 2**bit
        own = jnp.sum(jnp.where(stretch // 2**bit == block, spans, 0.0), axis=0)
        peer = jnp.sum(jnp.where(stretch // 2**bit == (block ^ 1), spans, 0.0), axis=0)
        own_spans.append(own)
        peer_spans.append(peer)
        offsets.append(offset)
        offset = offset + jnp.where(block % 2 == 1, peer, 0.0)
    return own_spans, peer_spans, offsets


Z_BITS = 4


class Side:
    def __init__(self, keep, pull, shard_index):
        keep, pull, shard_index = lax.optimization_barrier((keep, pull, shard_index))
        self.given = (keep, pull, shard_index)
        self.keep, self.pull = (
            [factor[:, None, None] for factor in factors] for factors in (keep, pull)
        )
        self.place = shard_index % 2

    def join(self, bit, block, peer):
        return self.keep[bit] * block + self.pull[bit] * peer


class Up(Side):
    def part(self, value, place):
        half = value.shape[0] // 2
        return lax.dynamic_slice_in_dim(value, place * half, half, axis=0)

    def mine(self, value):
        return self.part(value, self.place)

    def join_half(self, bit, block, peer):
        return self.mine(self.keep[bit]) * block + self.mine(self.pull[bit]) * peer

    def whole(self, own_half, other_half):
        ring = jnp.concatenate([own_half, other_half, own_half], axis=0)
        half = own_half.shape[0]
        return lax.dynamic_slice_in_dim(ring, self.place * half, 2 * half, axis=0)


class Down(Side):
    def mine(self, value):
        half = value.shape[1] // 2
        return jnp.where(self.place == 1, value[:, half:], value[:, :half])

    def theirs(self, value):
        half = value.shape[1] // 2
        return jnp.where(self.place == 1, value[:, :half], value[:, half:])

    def whole(self, own_half, other_half):
        ahead = jnp.concatenate([own_half, other_half], axis=1)
        behind = jnp.concatenate([other_half, own_half], axis=1)
        return jnp.where(self.place == 1, behind, ahead)


def mixer(seq_inputs, state_write, state_read, log_decay, level_weight, grad_out):
    row_count = seq_inputs.shape[0]
    head_count = log_decay.shape[0]
    head_width = seq_inputs.shape[1] // head_count
    inputs = seq_inputs.reshape(row_count, head_count, head_width)
    cotangent = grad_out.reshape(row_count, head_count, head_width)
    scaled = level_weight.astype(jnp.float32) * 0.125
    running = jnp.cumsum(log_decay, axis=1)
    total = running[:, -1]
    shard_index = lax.axis_index("ctx")
    level_count = lax.axis_size("ctx").bit_length() - 1
    own_spans, peer_spans, offsets = block_spans(total, shard_index, level_count)
    is_right = [shard_index // 2**bit % 2 == 1 for bit in range(level_count)]
    keep = [
        jnp.where(is_right[bit], 1.0, jnp.exp(peer_spans[bit])) for bit in range(level_count)
    ]
    pull = [jnp.where(is_right[bit], jnp.exp(own_spans[bit]), 1.0) for bit in range(level_count)]
    up = Up(keep, pull, shard_index)
    down = Down(*up.given)

    to_end = jnp.exp(total[:, None] - running)
    written = (to_end[:, :, None] * state_write.astype(jnp.float32)[None]).astype(jnp.bfloat16)
    state = jnp.einsum("uhp,hun->hpn", inputs, written, preferred_element_type=jnp.float32)
    coefficients, weighted, level_grads = ([], [], [])
    for bit in range(level_count):
        coeff = jnp.where(
            is_right[bit], scaled[bit + 1] * jnp.exp(running + offsets[bit][:, None]), 0.0
        )
        coefficients.append(coeff.T[:, :, None])
        weighted.append((coefficients[bit] * cotangent.astype(jnp.float32)).astype(jnp.bfloat16))
        level_grads.append(
            jnp.einsum("thp,tn->hpn", weighted[bit], state_read, preferred_element_type=jnp.float32)
        )
    buckets = [exchange(state, 0)]
    pair_state = up.join(0, state, buckets[0])
    half_state = up.mine(pair_state)
    half_buckets = []
    for bit in range(1, Z_BITS):
        half_buckets.append(exchange(half_state, bit))
        half_state = up.join_half(bit, half_state, half_buckets[-1])
    early = exchange(jnp.stack(half_buckets[:-1]), 0)
    late = exchange(half_buckets[-1], 0)
    block_state = pair_state
    for bit in range(1, Z_BITS):
        other_half = late if bit == Z_BITS - 1 else early[bit - 1]
        buckets.append(up.whole(half_buckets[bit - 1], other_half))
        block_state = up.join(bit, block_state, buckets[bit])
    for bit in range(Z_BITS, level_count):
        buckets.append(exchange(block_state, bit))
        if bit + 1 < level_count:
            block_state = up.join(bit, block_state, buckets[bit])
    carried = jnp.zeros_like(state)

    def step_down(bit, carried, level_grad):
        incoming = exchange(down.pull[bit] * carried + level_grad, bit)
        return down.keep[bit] * carried + incoming

    first_grads = to_left(level_grads[0])
    half_grads = exchange(jnp.stack([down.theirs(level_grads[bit]) for bit in range(1, Z_BITS)]), 0)
    for bit in reversed(range(Z_BITS, level_count)):
        carried = step_down(bit, carried, level_grads[bit])
    half_carried = down.mine(carried) + exchange(down.theirs(carried), 0)
    for bit in reversed(range(1, Z_BITS)):
        half_grad = down.mine(level_grads[bit]) + half_grads[bit - 1]
        half_carried = step_down(bit, half_carried, half_grad)
    pair_grad = down.whole(half_carried, exchange(half_carried, 0))
    dstate = down.keep[0] * pair_grad + first_grads
    scores = jnp.dot(state_read, state_write.T, preferred_element_type=jnp.float32)
    token_positions = jnp.arange(row_count)
    causal = (token_positions[:, None] >= token_positions[None, :])[None]
    gaps = running[:, :, None] - running[:, None, :]
    local_weight = (
        jnp.where(causal, jnp.exp(jnp.where(causal, gaps, 0.0)), 0.0) * scaled[0][:, :, None]
    )
    mixing = (local_weight * scores[None]).astype(jnp.bfloat16)
    y_local = jnp.einsum("htu,uhp->thp", mixing, inputs, preferred_element_type=jnp.float32)
    d_mixing = jnp.einsum("thp,uhp->htu", cotangent, inputs, preferred_element_type=jnp.float32)
    d_scores = (d_mixing * local_weight).astype(jnp.bfloat16)
    dread_local = jnp.einsum("htu,un->tn", d_scores, state_write, preferred_element_type=jnp.float32)
    dwrite_local = jnp.einsum("htu,tn->un", d_scores, state_read, preferred_element_type=jnp.float32)
    dinput_local = jnp.einsum("htu,thp->uhp", mixing, cotangent, preferred_element_type=jnp.float32)
    read_wide = state_read.astype(jnp.float32)
    y_far = jnp.zeros((row_count, head_count, head_width), jnp.float32)
    dread_far = jnp.zeros((row_count, state_read.shape[1]), jnp.float32)
    for bit in range(level_count):
        raw = jnp.einsum("tn,hpn->thp", read_wide, buckets[bit], precision=lax.Precision.HIGHEST)
        y_far = y_far + raw * coefficients[bit]
        dread_far = dread_far + jnp.einsum(
            "thp,hpn->tn",
            weighted[bit].astype(jnp.float32),
            buckets[bit],
            precision=lax.Precision.HIGHEST,
        )
    mixer_out = (y_local + y_far).astype(jnp.bfloat16).reshape(row_count, head_count * head_width)
    dstate_low = dstate.astype(jnp.bfloat16)
    dinput_far = jnp.einsum("hpn,hun->uhp", dstate_low, written, preferred_element_type=jnp.float32)
    per_head = jnp.einsum("hpn,uhp->uhn", dstate_low, inputs, preferred_element_type=jnp.float32)
    dwrite_far = jnp.sum(to_end.T[:, :, None] * per_head, axis=1)
    grad_inputs = (
        (dinput_local + dinput_far).astype(jnp.bfloat16).reshape(row_count, head_count * head_width)
    )
    grad_read = sum_at_owner(dread_local + dread_far, "head")
    grad_write = sum_at_owner(dwrite_local + dwrite_far, "head")
    return (mixer_out, grad_inputs, grad_write, grad_read)


def solution(mesh):
    return jax.shard_map(
        mixer,
        mesh=mesh,
        in_specs=(
            P("ctx", "head"),
            P("ctx", None),
            P("ctx", None),
            P("head", "ctx"),
            P(None, "head", "ctx"),
            P("ctx", "head"),
        ),
        out_specs=(
            P("ctx", "head"),
            P("ctx", "head"),
            P(("ctx", "head"), None),
            P(("ctx", "head"), None),
        ),
        check_vma=False,
    )
```

```python
import jax
import jax.numpy as jnp
from jax import lax
from jax.sharding import PartitionSpec as P


def exchange(value, bit):
    pairs = [(source, source ^ 2**bit) for source in range(lax.axis_size("ctx"))]
    return lax.ppermute(value, "ctx", pairs)


def to_left(value):
    pairs = [(source, source - 1) for source in range(1, lax.axis_size("ctx"), 2)]
    return lax.ppermute(value, "ctx", pairs)


def sum_at_owner(value, axis):
    pieces = value.reshape(lax.axis_size(axis), -1, value.shape[1])
    arrived = lax.all_to_all(pieces, axis, split_axis=0, concat_axis=0, tiled=True)
    return arrived.sum(axis=0)


def all_totals(total, groups):
    mine = jnp.broadcast_to(total[None, None, :], (len(groups[0]), 1, total.shape[0]))
    got = lax.all_to_all(mine, "ctx", 0, 0, axis_index_groups=groups, tiled=True)
    return got[:, 0]


def sum_where(mask, spans):
    return jnp.sum(jnp.where(mask[:, None], spans, 0.0), axis=0)


def sibling_spans(spans, position):
    member = jnp.arange(spans.shape[0])
    levels = []
    offset = jnp.zeros_like(spans[0])
    for bit in range(spans.shape[0].bit_length() - 1):
        block = position // 2**bit
        own = sum_where(member // 2**bit == block, spans)
        peer = sum_where(member // 2**bit == (block ^ 1), spans)
        levels.append((own, peer, offset))
        offset = offset + jnp.where(block % 2 == 1, peer, 0.0)
    return levels, offset


Z_BITS = 4

GATHERS = ((1, 2, 3), (4, 5), (6,))


class Side:
    def __init__(self, *stages):
        self.given = tuple(lax.optimization_barrier(stage) for stage in stages)
        self.place = self.given[0][2]
        self.keep, self.pull = (
            [factor[:, None, None] for stage in self.given for factor in stage[part]]
            for part in (0, 1)
        )

    def join(self, bit, block, peer):
        return self.keep[bit] * block + self.pull[bit] * peer


class Up(Side):
    def part(self, value, place):
        half = value.shape[0] // 2
        return lax.dynamic_slice_in_dim(value, place * half, half, axis=0)

    def mine(self, value):
        return self.part(value, self.place)

    def join_half(self, bit, block, peer):
        return self.mine(self.keep[bit]) * block + self.mine(self.pull[bit]) * peer

    def whole(self, own_half, other_half):
        ring = jnp.concatenate([own_half, other_half, own_half], axis=0)
        half = own_half.shape[0]
        return lax.dynamic_slice_in_dim(ring, self.place * half, 2 * half, axis=0)


def other_half(value, place):
    half = value.shape[1] // 2
    return jnp.where(place == 1, value[:, :half], value[:, half:])


class Down(Side):
    def mine(self, value):
        half = value.shape[1] // 2
        return jnp.where(self.place == 1, value[:, half:], value[:, :half])

    def theirs(self, value):
        return other_half(value, self.place)

    def whole(self, own_half, other_half):
        ahead = jnp.concatenate([own_half, other_half], axis=1)
        behind = jnp.concatenate([other_half, own_half], axis=1)
        return jnp.where(self.place == 1, behind, ahead)


def mixer(seq_inputs, state_write, state_read, log_decay, level_weight, grad_out):
    row_count = seq_inputs.shape[0]
    head_count = log_decay.shape[0]
    head_width = seq_inputs.shape[1] // head_count
    inputs = seq_inputs.reshape(row_count, head_count, head_width)
    cotangent = grad_out.reshape(row_count, head_count, head_width)
    scaled = level_weight.astype(jnp.float32) * 0.125
    running = jnp.cumsum(log_decay, axis=1)
    total = running[:, -1]
    shard_index = lax.axis_index("ctx")
    level_count = lax.axis_size("ctx").bit_length() - 1
    ring = 2**Z_BITS
    rows = 2 ** (level_count - Z_BITS)
    along_z = [[row * ring + place for place in range(ring)] for row in range(rows)]
    along_y = [[row * ring + place for row in range(rows)] for place in range(ring)]
    z_place, y_place = (shard_index % ring, shard_index // ring)
    z_spans = all_totals(total, along_z)
    is_right = [shard_index // 2**bit % 2 == 1 for bit in range(level_count)]

    def factors(levels, first_bit):
        right = is_right[first_bit : first_bit + len(levels)]
        keep = [jnp.where(r, 1.0, jnp.exp(peer)) for r, (_, peer, _) in zip(right, levels)]
        pull = [jnp.where(r, jnp.exp(own), 1.0) for r, (own, _, _) in zip(right, levels)]
        return keep, pull

    z_levels, z_prefix = sibling_spans(z_spans, z_place)
    member = jnp.arange(ring)
    own_reach = jnp.exp(sum_where(member < z_place, z_spans))
    peer_reach = jnp.exp(sum_where(member < (z_place ^ 1), z_spans))
    row_total = jnp.sum(z_spans, axis=0)
    z_factors, z_offsets, z_prefix, reaches, row_total = lax.optimization_barrier(
        (
            factors(z_levels, 0),
            [level[2] for level in z_levels],
            z_prefix,
            (own_reach, peer_reach),
            row_total,
        )
    )
    own_reach, peer_reach = (reach[:, None, None] for reach in reaches)
    y_spans = all_totals(row_total, along_y)
    y_levels, _ = sibling_spans(y_spans, y_place)
    offsets = z_offsets + [z_prefix + level[2] for level in y_levels]
    up = Up((*z_factors, shard_index % 2), factors(y_levels, Z_BITS))
    down = Down(*up.given)

    to_end = jnp.exp(total[:, None] - running)
    written = (to_end[:, :, None] * state_write.astype(jnp.float32)[None]).astype(jnp.bfloat16)
    state = jnp.einsum("uhp,hun->hpn", inputs, written, preferred_element_type=jnp.float32)

    def coefficient(level, log_reach, bit, place):
        right = place // 2**bit % 2 == 1
        return jnp.where(right, level * jnp.exp(log_reach), 0.0).T[:, :, None]

    def weigh(coeff):
        return (coeff * cotangent.astype(jnp.float32)).astype(jnp.bfloat16)

    def bucket_grad(part):
        return jnp.einsum("thp,tn->hpn", part, state_read, preferred_element_type=jnp.float32)

    near, far = (range(1, Z_BITS), range(Z_BITS, level_count))
    start = lax.optimization_barrier((running, scaled[Z_BITS + 1 :], shard_index))
    early_grads = {
        bit: bucket_grad(weigh(coefficient(start[1][bit - Z_BITS], start[0], bit, start[2])))
        for bit in far
    }
    early_sent = jnp.stack([other_half(early_grads[bit], start[2] % 2) for bit in far])
    coefficients, weighted = ([], [])
    *start, state, early_sent = lax.optimization_barrier((*start, state, early_sent))
    for bit in range(Z_BITS):
        log_reach = start[0] + offsets[bit][:, None] if bit else start[0]
        coefficients.append(coefficient(scaled[bit + 1], log_reach, bit, start[2]))
        weighted.append(weigh(coefficients[bit]))
    level_grads = [bucket_grad(part) for part in weighted]
    *start, row_offsets, coefficients = lax.optimization_barrier(
        (*start, offsets[Z_BITS:], coefficients)
    )
    for bit in far:
        log_reach = start[0] + row_offsets[bit - Z_BITS][:, None]
        coefficients.append(coefficient(start[1][bit - Z_BITS], log_reach, bit, start[2]))
        weighted.append(weigh(coefficients[bit]))
    buckets = {0: exchange(state, 0)}
    half_state = up.mine(up.join(0, state, buckets[0]))
    half_buckets = {}
    for bit in range(1, level_count):
        half_buckets[bit] = exchange(half_state, bit)
        half_state = up.join_half(bit, half_state, half_buckets[bit])
    for bits in GATHERS:
        others = exchange(jnp.stack([half_buckets[bit] for bit in bits]), 0)
        for place, bit in enumerate(bits):
            buckets[bit] = up.whole(half_buckets[bit], others[place])
    first_grads = to_left(level_grads[0])
    half_grads = {}
    others = exchange(jnp.stack([down.theirs(level_grads[bit]) for bit in near]), 0)
    for place, bit in enumerate(near):
        half_grads[bit] = down.mine(level_grads[bit]) + others[place]
    others = exchange(early_sent, 0)
    y_member = jnp.arange(rows)
    for place, bit in enumerate(far):
        half_grads[bit] = own_reach * down.mine(early_grads[bit]) + peer_reach * others[place]
    top = level_count - 1
    sender = y_place ^ (rows // 2)
    before = (y_member >= sender // (rows // 2) * (rows // 2)) & (y_member < sender)
    row_reach = jnp.exp(sum_where(before, y_spans))[:, None, None]
    half_carried = row_reach * exchange(half_grads[top], top)
    for bit in reversed(range(1, top)):
        grad = half_grads[bit]
        if bit >= Z_BITS:
            grad = jnp.exp(y_levels[bit - Z_BITS][2])[:, None, None] * grad
        incoming = exchange(grad + down.pull[bit] * half_carried, bit)
        half_carried = down.keep[bit] * half_carried + incoming
    pair_grad = down.whole(half_carried, exchange(half_carried, 0))
    dstate = down.keep[0] * pair_grad + first_grads
    scores = jnp.dot(state_read, state_write.T, preferred_element_type=jnp.float32)
    token_positions = jnp.arange(row_count)
    causal = (token_positions[:, None] >= token_positions[None, :])[None]
    gaps = running[:, :, None] - running[:, None, :]
    local_weight = (
        jnp.where(causal, jnp.exp(jnp.where(causal, gaps, 0.0)), 0.0) * scaled[0][:, :, None]
    )
    mixing = (local_weight * scores[None]).astype(jnp.bfloat16)
    y_local = jnp.einsum("htu,uhp->thp", mixing, inputs, preferred_element_type=jnp.float32)
    d_mixing = jnp.einsum("thp,uhp->htu", cotangent, inputs, preferred_element_type=jnp.float32)
    d_scores = (d_mixing * local_weight).astype(jnp.bfloat16)
    dread_local = jnp.einsum("htu,un->tn", d_scores, state_write, preferred_element_type=jnp.float32)
    dwrite_local = jnp.einsum("htu,tn->un", d_scores, state_read, preferred_element_type=jnp.float32)
    dinput_local = jnp.einsum("htu,thp->uhp", mixing, cotangent, preferred_element_type=jnp.float32)
    read_wide = state_read.astype(jnp.float32)
    y_far = jnp.zeros((row_count, head_count, head_width), jnp.float32)
    dread_far = jnp.zeros((row_count, state_read.shape[1]), jnp.float32)
    for bit in range(level_count):
        raw = jnp.einsum("tn,hpn->thp", read_wide, buckets[bit], precision=lax.Precision.HIGHEST)
        y_far = y_far + raw * coefficients[bit]
        dread_far = dread_far + jnp.einsum(
            "thp,hpn->tn",
            weighted[bit].astype(jnp.float32),
            buckets[bit],
            precision=lax.Precision.HIGHEST,
        )
    mixer_out = (y_local + y_far).astype(jnp.bfloat16).reshape(row_count, head_count * head_width)
    dstate_low = dstate.astype(jnp.bfloat16)
    dinput_far = jnp.einsum("hpn,hun->uhp", dstate_low, written, preferred_element_type=jnp.float32)
    per_head = jnp.einsum("hpn,uhp->uhn", dstate_low, inputs, preferred_element_type=jnp.float32)
    dwrite_far = jnp.sum(to_end.T[:, :, None] * per_head, axis=1)
    grad_inputs = (
        (dinput_local + dinput_far).astype(jnp.bfloat16).reshape(row_count, head_count * head_width)
    )
    grad_read = sum_at_owner(dread_local + dread_far, "head")
    grad_write = sum_at_owner(dwrite_local + dwrite_far, "head")
    return (mixer_out, grad_inputs, grad_write, grad_read)


def solution(mesh):
    return jax.shard_map(
        mixer,
        mesh=mesh,
        in_specs=(
            P("ctx", "head"),
            P("ctx", None),
            P("ctx", None),
            P("head", "ctx"),
            P(None, "head", "ctx"),
            P("ctx", "head"),
        ),
        out_specs=(
            P("ctx", "head"),
            P("ctx", "head"),
            P(("ctx", "head"), None),
            P(("ctx", "head"), None),
        ),
        check_vma=False,
    )
```

```python
import jax
import jax.numpy as jnp
from jax import lax
from jax.sharding import PartitionSpec as P


def exchange(value, bit):
    pairs = [(source, source ^ 2**bit) for source in range(lax.axis_size("ctx"))]
    return lax.ppermute(value, "ctx", pairs)


def to_left(value):
    pairs = [(source, source - 1) for source in range(1, lax.axis_size("ctx"), 2)]
    return lax.ppermute(value, "ctx", pairs)


def sum_at_owner(value, axis):
    pieces = value.reshape(lax.axis_size(axis), -1, value.shape[1])
    arrived = lax.all_to_all(pieces, axis, split_axis=0, concat_axis=0, tiled=True)
    return arrived.sum(axis=0)


def all_totals(total, groups):
    mine = jnp.broadcast_to(total[None, None, :], (len(groups[0]), 1, total.shape[0]))
    got = lax.all_to_all(mine, "ctx", 0, 0, axis_index_groups=groups, tiled=True)
    return got[:, 0]


def sum_where(mask, spans):
    return jnp.sum(jnp.where(mask[:, None], spans, 0.0), axis=0)


def sibling_spans(spans, position):
    member = jnp.arange(spans.shape[0])
    levels = []
    offset = jnp.zeros_like(spans[0])
    for bit in range(spans.shape[0].bit_length() - 1):
        block = position // 2**bit
        own = sum_where(member // 2**bit == block, spans)
        peer = sum_where(member // 2**bit == (block ^ 1), spans)
        levels.append((own, peer, offset))
        offset = offset + jnp.where(block % 2 == 1, peer, 0.0)
    return levels, offset


Z_BITS = 4

GATHERS = ((1, 2, 3), (4, 5), (6,))


class Side:
    def __init__(self, *stages):
        self.given = tuple(lax.optimization_barrier(stage) for stage in stages)
        self.place = self.given[0][2]
        self.keep, self.pull = (
            [factor[:, None, None] for stage in self.given for factor in stage[part]]
            for part in (0, 1)
        )

    def join(self, bit, block, peer):
        return self.keep[bit] * block + self.pull[bit] * peer


class Up(Side):
    def part(self, value, place):
        half = value.shape[0] // 2
        return lax.dynamic_slice_in_dim(value, place * half, half, axis=0)

    def mine(self, value):
        return self.part(value, self.place)

    def join_half(self, bit, block, peer):
        return self.mine(self.keep[bit]) * block + self.mine(self.pull[bit]) * peer

    def whole(self, own_half, other_half):
        ring = jnp.concatenate([own_half, other_half, own_half], axis=0)
        half = own_half.shape[0]
        return lax.dynamic_slice_in_dim(ring, self.place * half, 2 * half, axis=0)


def other_half(value, place):
    half = value.shape[1] // 2
    return jnp.where(place == 1, value[:, :half], value[:, half:])


class Down(Side):
    def mine(self, value):
        half = value.shape[1] // 2
        return jnp.where(self.place == 1, value[:, half:], value[:, :half])

    def theirs(self, value):
        return other_half(value, self.place)

    def whole(self, own_half, other_half):
        ahead = jnp.concatenate([own_half, other_half], axis=1)
        behind = jnp.concatenate([other_half, own_half], axis=1)
        return jnp.where(self.place == 1, behind, ahead)


def mixer(seq_inputs, state_write, state_read, log_decay, level_weight, grad_out):
    row_count = seq_inputs.shape[0]
    head_count = log_decay.shape[0]
    head_width = seq_inputs.shape[1] // head_count
    inputs = seq_inputs.reshape(row_count, head_count, head_width)
    cotangent = grad_out.reshape(row_count, head_count, head_width)
    scaled = level_weight.astype(jnp.float32) * 0.125
    running = jnp.cumsum(log_decay, axis=1)
    total = running[:, -1]
    shard_index = lax.axis_index("ctx")
    level_count = lax.axis_size("ctx").bit_length() - 1
    ring = 2**Z_BITS
    rows = 2 ** (level_count - Z_BITS)
    along_z = [[row * ring + place for place in range(ring)] for row in range(rows)]
    along_y = [[row * ring + place for row in range(rows)] for place in range(ring)]
    z_place, y_place = (shard_index % ring, shard_index // ring)
    z_spans = all_totals(total, along_z)
    is_right = [shard_index // 2**bit % 2 == 1 for bit in range(level_count)]

    def factors(levels, first_bit):
        right = is_right[first_bit : first_bit + len(levels)]
        keep = [jnp.where(r, 1.0, jnp.exp(peer)) for r, (_, peer, _) in zip(right, levels)]
        pull = [jnp.where(r, jnp.exp(own), 1.0) for r, (own, _, _) in zip(right, levels)]
        return keep, pull

    z_levels, z_prefix = sibling_spans(z_spans, z_place)
    row_total = jnp.sum(z_spans, axis=0)
    z_factors, z_offsets, z_prefix, row_total = lax.optimization_barrier(
        (
            factors(z_levels, 0),
            [level[2] for level in z_levels],
            z_prefix,
            row_total,
        )
    )
    y_spans = all_totals(row_total, along_y)
    y_levels, _ = sibling_spans(y_spans, y_place)
    offsets = z_offsets + [z_prefix + level[2] for level in y_levels]
    up = Up((*z_factors, shard_index % 2), factors(y_levels, Z_BITS))
    down = Down(*up.given)

    to_end = jnp.exp(total[:, None] - running)
    written = (to_end[:, :, None] * state_write.astype(jnp.float32)[None]).astype(jnp.bfloat16)
    state = jnp.einsum("uhp,hun->hpn", inputs, written, preferred_element_type=jnp.float32)

    def coefficient(level, log_reach, bit, place):
        right = place // 2**bit % 2 == 1
        return jnp.where(right, level * jnp.exp(log_reach), 0.0).T[:, :, None]

    def weigh(coeff):
        return (coeff * cotangent.astype(jnp.float32)).astype(jnp.bfloat16)

    def bucket_grad(part):
        return jnp.einsum("thp,tn->hpn", part, state_read, preferred_element_type=jnp.float32)

    far = range(Z_BITS, level_count)
    coefficients, weighted = ([], [])
    *start, state = lax.optimization_barrier(
        (running, scaled[Z_BITS + 1 :], shard_index, state)
    )
    for bit in range(Z_BITS):
        log_reach = start[0] + offsets[bit][:, None] if bit else start[0]
        coefficients.append(coefficient(scaled[bit + 1], log_reach, bit, start[2]))
        weighted.append(weigh(coefficients[bit]))
    level_grads = [bucket_grad(part) for part in weighted]
    *start, row_offsets, coefficients = lax.optimization_barrier(
        (*start, offsets[Z_BITS:], coefficients)
    )
    for bit in far:
        log_reach = start[0] + row_offsets[bit - Z_BITS][:, None]
        coefficients.append(coefficient(start[1][bit - Z_BITS], log_reach, bit, start[2]))
        weighted.append(weigh(coefficients[bit]))
        level_grads.append(bucket_grad(weighted[bit]))
    buckets = {0: exchange(state, 0)}
    half_state = up.mine(up.join(0, state, buckets[0]))
    half_buckets = {}
    for bit in range(1, level_count):
        half_buckets[bit] = exchange(half_state, bit)
        half_state = up.join_half(bit, half_state, half_buckets[bit])
    for bits in GATHERS:
        others = exchange(jnp.stack([half_buckets[bit] for bit in bits]), 0)
        for place, bit in enumerate(bits):
            buckets[bit] = up.whole(half_buckets[bit], others[place])
    first_grads = to_left(level_grads[0])
    half_grads = {}
    for bits in GATHERS:
        sent = jnp.stack([down.theirs(level_grads[bit]) for bit in bits])
        others = exchange(sent, 0)
        for place, bit in enumerate(bits):
            half_grads[bit] = down.mine(level_grads[bit]) + others[place]
    half_carried = jnp.zeros_like(half_grads[1])
    for bit in reversed(range(1, level_count)):
        incoming = exchange(half_grads[bit] + down.pull[bit] * half_carried, bit)
        half_carried = down.keep[bit] * half_carried + incoming
    pair_grad = down.whole(half_carried, exchange(half_carried, 0))
    dstate = down.keep[0] * pair_grad + first_grads
    scores = jnp.dot(state_read, state_write.T, preferred_element_type=jnp.float32)
    token_positions = jnp.arange(row_count)
    causal = (token_positions[:, None] >= token_positions[None, :])[None]
    gaps = running[:, :, None] - running[:, None, :]
    local_weight = (
        jnp.where(causal, jnp.exp(jnp.where(causal, gaps, 0.0)), 0.0) * scaled[0][:, :, None]
    )
    mixing = (local_weight * scores[None]).astype(jnp.bfloat16)
    y_local = jnp.einsum("htu,uhp->thp", mixing, inputs, preferred_element_type=jnp.float32)
    d_mixing = jnp.einsum("thp,uhp->htu", cotangent, inputs, preferred_element_type=jnp.float32)
    d_scores = (d_mixing * local_weight).astype(jnp.bfloat16)
    dread_local = jnp.einsum("htu,un->tn", d_scores, state_write, preferred_element_type=jnp.float32)
    dwrite_local = jnp.einsum("htu,tn->un", d_scores, state_read, preferred_element_type=jnp.float32)
    dinput_local = jnp.einsum("htu,thp->uhp", mixing, cotangent, preferred_element_type=jnp.float32)
    read_wide = state_read.astype(jnp.float32)
    y_far = jnp.zeros((row_count, head_count, head_width), jnp.float32)
    dread_far = jnp.zeros((row_count, state_read.shape[1]), jnp.float32)
    for bit in range(level_count):
        raw = jnp.einsum("tn,hpn->thp", read_wide, buckets[bit], precision=lax.Precision.HIGHEST)
        y_far = y_far + raw * coefficients[bit]
        dread_far = dread_far + jnp.einsum(
            "thp,hpn->tn",
            weighted[bit].astype(jnp.float32),
            buckets[bit],
            precision=lax.Precision.HIGHEST,
        )
    mixer_out = (y_local + y_far).astype(jnp.bfloat16).reshape(row_count, head_count * head_width)
    dstate_low = dstate.astype(jnp.bfloat16)
    dinput_far = jnp.einsum("hpn,hun->uhp", dstate_low, written, preferred_element_type=jnp.float32)
    per_head = jnp.einsum("hpn,uhp->uhn", dstate_low, inputs, preferred_element_type=jnp.float32)
    dwrite_far = jnp.sum(to_end.T[:, :, None] * per_head, axis=1)
    grad_inputs = (
        (dinput_local + dinput_far).astype(jnp.bfloat16).reshape(row_count, head_count * head_width)
    )
    grad_read = sum_at_owner(dread_local + dread_far, "head")
    grad_write = sum_at_owner(dwrite_local + dwrite_far, "head")
    return (mixer_out, grad_inputs, grad_write, grad_read)


def solution(mesh):
    return jax.shard_map(
        mixer,
        mesh=mesh,
        in_specs=(
            P("ctx", "head"),
            P("ctx", None),
            P("ctx", None),
            P("head", "ctx"),
            P(None, "head", "ctx"),
            P("ctx", "head"),
        ),
        out_specs=(
            P("ctx", "head"),
            P("ctx", "head"),
            P(("ctx", "head"), None),
            P(("ctx", "head"), None),
        ),
        check_vma=False,
    )
```

```python
import jax
import jax.numpy as jnp
from jax import lax
from jax.sharding import PartitionSpec as P


def exchange(value, bit):
    pairs = [(source, source ^ 2**bit) for source in range(lax.axis_size("ctx"))]
    return lax.ppermute(value, "ctx", pairs)


def to_left(value):
    pairs = [(source, source - 1) for source in range(1, lax.axis_size("ctx"), 2)]
    return lax.ppermute(value, "ctx", pairs)


def sum_at_owner(value, axis):
    pieces = value.reshape(lax.axis_size(axis), -1, value.shape[1])
    return lax.all_to_all(pieces, axis, split_axis=0, concat_axis=0, tiled=True).sum(axis=0)


def all_totals(total, groups):
    mine = jnp.broadcast_to(total[None, None, :], (len(groups[0]), 1, total.shape[0]))
    got = lax.all_to_all(mine, "ctx", 0, 0, axis_index_groups=groups, tiled=True)
    return got[:, 0]


def block_spans(total, shard_index, level_count):
    ring = 2**Z_BITS
    rows = 2 ** (level_count - Z_BITS)
    along_z = [[row * ring + place for place in range(ring)] for row in range(rows)]
    along_y = [[row * ring + place for row in range(rows)] for place in range(ring)]
    own_spans, peer_spans, offsets = ([], [], [])
    offset = jnp.zeros_like(total)
    for groups, position in ((along_z, shard_index % ring), (along_y, shard_index // ring)):
        spans = all_totals(total, groups)
        member = jnp.arange(spans.shape[0])[:, None]
        for bit in range(spans.shape[0].bit_length() - 1):
            block = position // 2**bit
            own = jnp.sum(jnp.where(member // 2**bit == block, spans, 0.0), axis=0)
            peer = jnp.sum(jnp.where(member // 2**bit == (block ^ 1), spans, 0.0), axis=0)
            own_spans.append(own)
            peer_spans.append(peer)
            offsets.append(offset)
            offset = offset + jnp.where(block % 2 == 1, peer, 0.0)
        total = jnp.sum(spans, axis=0)
    return own_spans, peer_spans, offsets


Z_BITS = 4

GATHERS = ((1, 2, 3), (4, 5), (6,))


class Side:
    def __init__(self, keep, pull, shard_index):
        keep, pull, shard_index = lax.optimization_barrier((keep, pull, shard_index))
        self.given = (keep, pull, shard_index)
        self.keep, self.pull = (
            [factor[:, None, None] for factor in factors] for factors in (keep, pull)
        )
        self.place = shard_index % 2

    def join(self, bit, block, peer):
        return self.keep[bit] * block + self.pull[bit] * peer


class Up(Side):
    def part(self, value, place):
        half = value.shape[0] // 2
        return lax.dynamic_slice_in_dim(value, place * half, half, axis=0)

    def mine(self, value):
        return self.part(value, self.place)

    def join_half(self, bit, block, peer):
        return self.mine(self.keep[bit]) * block + self.mine(self.pull[bit]) * peer

    def whole(self, own_half, other_half):
        ring = jnp.concatenate([own_half, other_half, own_half], axis=0)
        half = own_half.shape[0]
        return lax.dynamic_slice_in_dim(ring, self.place * half, 2 * half, axis=0)


class Down(Side):
    def mine(self, value):
        half = value.shape[1] // 2
        return jnp.where(self.place == 1, value[:, half:], value[:, :half])

    def theirs(self, value):
        half = value.shape[1] // 2
        return jnp.where(self.place == 1, value[:, :half], value[:, half:])

    def whole(self, own_half, other_half):
        ahead = jnp.concatenate([own_half, other_half], axis=1)
        behind = jnp.concatenate([other_half, own_half], axis=1)
        return jnp.where(self.place == 1, behind, ahead)


def mixer(seq_inputs, state_write, state_read, log_decay, level_weight, grad_out):
    row_count = seq_inputs.shape[0]
    head_count = log_decay.shape[0]
    head_width = seq_inputs.shape[1] // head_count
    inputs = seq_inputs.reshape(row_count, head_count, head_width)
    cotangent = grad_out.reshape(row_count, head_count, head_width)
    scaled = level_weight.astype(jnp.float32) * 0.125
    running = jnp.cumsum(log_decay, axis=1)
    total = running[:, -1]
    shard_index = lax.axis_index("ctx")
    level_count = lax.axis_size("ctx").bit_length() - 1
    own_spans, peer_spans, offsets = block_spans(total, shard_index, level_count)
    is_right = [shard_index // 2**bit % 2 == 1 for bit in range(level_count)]
    keep = [
        jnp.where(is_right[bit], 1.0, jnp.exp(peer_spans[bit])) for bit in range(level_count)
    ]
    pull = [jnp.where(is_right[bit], jnp.exp(own_spans[bit]), 1.0) for bit in range(level_count)]
    up = Up(keep, pull, shard_index)
    down = Down(*up.given)

    to_end = jnp.exp(total[:, None] - running)
    written = (to_end[:, :, None] * state_write.astype(jnp.float32)[None]).astype(jnp.bfloat16)
    state = jnp.einsum("uhp,hun->hpn", inputs, written, preferred_element_type=jnp.float32)
    coefficients, weighted, level_grads = ([], [], [])
    for bit in range(level_count):
        coeff = jnp.where(
            is_right[bit], scaled[bit + 1] * jnp.exp(running + offsets[bit][:, None]), 0.0
        )
        coefficients.append(coeff.T[:, :, None])
        weighted.append((coefficients[bit] * cotangent.astype(jnp.float32)).astype(jnp.bfloat16))
        level_grads.append(
            jnp.einsum("thp,tn->hpn", weighted[bit], state_read, preferred_element_type=jnp.float32)
        )
    buckets = {0: exchange(state, 0)}
    half_state = up.mine(up.join(0, state, buckets[0]))
    half_buckets = {}
    for bit in range(1, level_count):
        half_buckets[bit] = exchange(half_state, bit)
        half_state = up.join_half(bit, half_state, half_buckets[bit])
    for bits in GATHERS:
        others = exchange(jnp.stack([half_buckets[bit] for bit in bits]), 0)
        for place, bit in enumerate(bits):
            buckets[bit] = up.whole(half_buckets[bit], others[place])
    first_grads = to_left(level_grads[0])
    half_grads = {}
    for bits in GATHERS:
        sent = jnp.stack([down.theirs(level_grads[bit]) for bit in bits])
        others = exchange(sent, 0)
        for place, bit in enumerate(bits):
            half_grads[bit] = down.mine(level_grads[bit]) + others[place]
    half_carried = jnp.zeros_like(half_grads[1])
    for bit in reversed(range(1, level_count)):
        incoming = exchange(half_grads[bit] + down.pull[bit] * half_carried, bit)
        half_carried = down.keep[bit] * half_carried + incoming
    pair_grad = down.whole(half_carried, exchange(half_carried, 0))
    dstate = down.keep[0] * pair_grad + first_grads
    scores = jnp.dot(state_read, state_write.T, preferred_element_type=jnp.float32)
    token_positions = jnp.arange(row_count)
    causal = (token_positions[:, None] >= token_positions[None, :])[None]
    gaps = running[:, :, None] - running[:, None, :]
    local_weight = (
        jnp.where(causal, jnp.exp(jnp.where(causal, gaps, 0.0)), 0.0) * scaled[0][:, :, None]
    )
    mixing = (local_weight * scores[None]).astype(jnp.bfloat16)
    y_local = jnp.einsum("htu,uhp->thp", mixing, inputs, preferred_element_type=jnp.float32)
    d_mixing = jnp.einsum("thp,uhp->htu", cotangent, inputs, preferred_element_type=jnp.float32)
    d_scores = (d_mixing * local_weight).astype(jnp.bfloat16)
    dread_local = jnp.einsum("htu,un->tn", d_scores, state_write, preferred_element_type=jnp.float32)
    dwrite_local = jnp.einsum("htu,tn->un", d_scores, state_read, preferred_element_type=jnp.float32)
    dinput_local = jnp.einsum("htu,thp->uhp", mixing, cotangent, preferred_element_type=jnp.float32)
    read_wide = state_read.astype(jnp.float32)
    y_far = jnp.zeros((row_count, head_count, head_width), jnp.float32)
    dread_far = jnp.zeros((row_count, state_read.shape[1]), jnp.float32)
    for bit in range(level_count):
        raw = jnp.einsum("tn,hpn->thp", read_wide, buckets[bit], precision=lax.Precision.HIGHEST)
        y_far = y_far + raw * coefficients[bit]
        dread_far = dread_far + jnp.einsum(
            "thp,hpn->tn",
            weighted[bit].astype(jnp.float32),
            buckets[bit],
            precision=lax.Precision.HIGHEST,
        )
    mixer_out = (y_local + y_far).astype(jnp.bfloat16).reshape(row_count, head_count * head_width)
    dstate_low = dstate.astype(jnp.bfloat16)
    dinput_far = jnp.einsum("hpn,hun->uhp", dstate_low, written, preferred_element_type=jnp.float32)
    per_head = jnp.einsum("hpn,uhp->uhn", dstate_low, inputs, preferred_element_type=jnp.float32)
    dwrite_far = jnp.sum(to_end.T[:, :, None] * per_head, axis=1)
    grad_inputs = (
        (dinput_local + dinput_far).astype(jnp.bfloat16).reshape(row_count, head_count * head_width)
    )
    both = jnp.concatenate([dwrite_local + dwrite_far, dread_local + dread_far], axis=1)
    grad_write, grad_read = jnp.split(sum_at_owner(both, "head"), 2, axis=1)
    return (mixer_out, grad_inputs, grad_write, grad_read)


def solution(mesh):
    return jax.shard_map(
        mixer,
        mesh=mesh,
        in_specs=(
            P("ctx", "head"),
            P("ctx", None),
            P("ctx", None),
            P("head", "ctx"),
            P(None, "head", "ctx"),
            P("ctx", "head"),
        ),
        out_specs=(
            P("ctx", "head"),
            P("ctx", "head"),
            P(("ctx", "head"), None),
            P(("ctx", "head"), None),
        ),
        check_vma=False,
    )
```
